32 devices in a mesh: tm: 4 (over z), tile: 8 (over y, x, core).
Axes of the slice: x: 2, y: 2, z: 4, core: 2. Of those that a mesh axis runs over, the one named last changes fastest.
Arguments:
- frames: bfloat16 [1024, 49152], P('tm', 'tile'), may hold values from -16 to 16
- segments: int32 [1024], replicated, may hold values from 0 to 2, as said below
- offset: int32 [1], replicated, may hold values from 0 to 45056
Outputs:
- instant: float32 [4096, 49152], P('tm', 'tile')
- lagged: float32 [4096, 49152], P('tm', 'tile')
The draws below stay inside these ranges and needn't reach their ends.
Inputs may be any that keep to these rules, and one draw needn't show every extreme that they name: `segments`: each trajectory is a run of frames, in order of its id.
All inputs are finite; a program needn't handle non-finite values.
Results may differ from the reference program's by a relative error of at most 0.0036.
Values may be sent and summed in bfloat16 or wider, within the bound.
A program may use at most 128 MiB of HBM per device.

```python
import math
import jax
import jax.numpy as jnp
from jax import lax

F = 49152
S = 4096
LAG = 256
FRAMES = 1024


def draw_frames(key, part):
    keys = jax.random.split(key, 7)
    times = jnp.arange(FRAMES, dtype=jnp.float32)[:, None]
    drift = jax.random.normal(keys[0], (1, F), jnp.float32)
    first_load = jax.random.normal(keys[1], (1, F), jnp.float32)
    second_load = jax.random.normal(keys[2], (1, F), jnp.float32)
    period = jax.random.uniform(keys[3], (), jnp.float32, 2.0 * LAG, 6.0 * LAG)
    phase = jax.random.uniform(keys[4], (), jnp.float32, -math.pi, math.pi)
    slow = 1.4 * jnp.cos(2.0 * math.pi * times / period + phase)
    rough = jax.random.normal(keys[5], (FRAMES, 1), jnp.float32)
    noise = jax.random.normal(keys[6], (FRAMES, F), jnp.float32)
    values = 0.8 * drift * (1.0 + 2.0 * times / FRAMES) + first_load * slow + 0.7 * second_load * rough + noise
    return jnp.clip(values, -16.0, 16.0).astype(jnp.bfloat16)


def draw_segments(key, part):
    keys = jax.random.split(jax.random.fold_in(key, 11), 2)
    first_end = jax.random.randint(keys[0], (), FRAMES // 8, FRAMES // 4, jnp.int32)
    second_end = jax.random.randint(keys[1], (), 5 * FRAMES // 8, 3 * FRAMES // 4, jnp.int32)
    stamps = jnp.arange(FRAMES, dtype=jnp.int32)
    return (stamps >= first_end).astype(jnp.int32) + (stamps >= second_end).astype(jnp.int32)


def setup_inputs(seed: int = 0) -> dict:
    seeds = jax.random.split(jax.random.key(seed), 4)
    return {
        "frames": draw_frames(jax.random.fold_in(seeds[3], 71), 0),
        "segments": draw_segments(jax.random.fold_in(seeds[3], 71), 0),
        "offset": jax.random.randint(seeds[2], (1,), 0, F - S + 1).astype(jnp.int32),
    }


def reference(frames, segments, offset):
    total = frames.shape[0]
    mean = jnp.sum(frames.astype(jnp.float32), axis=0) / total
    centered = (frames.astype(jnp.float32) - mean).astype(jnp.bfloat16)
    slab = lax.dynamic_slice_in_dim(centered, offset[0].astype(jnp.int32), S, 1)
    dims = (((0,), (0,)), ((), ()))
    instant = lax.dot_general(slab, centered, dims, preferred_element_type=jnp.float32) / total
    count = total - LAG
    valid = (segments[:count] == segments[LAG:]).astype(jnp.bfloat16)[:, None]
    pairs = jnp.sum(valid.astype(jnp.float32))
    left = jnp.concatenate([slab[:count], slab[LAG:]], axis=0)
    right = jnp.concatenate([centered[LAG:] * valid, centered[:count] * valid], axis=0)
    lagged = lax.dot_general(left, right, dims, preferred_element_type=jnp.float32) * 0.5 / pairs
    return instant, lagged
```

```python
import functools

import jax
import jax.numpy as jnp
from jax import lax
from jax.experimental import pallas as pl
from jax.experimental.pallas import tpu as pltpu
from jax.sharding import PartitionSpec as P


S = 4096
LAG = 256
BLOCK = 256
UNITS = (7, 7, 5, 3, 2)


def chunk_kernel(total, z_ref, scale_ref, st_ref, lt_ref, own_ref, near_ref, far_ref, inner_ref, outer_ref, *rest):
    inst_ref, lag_ref, xs = rest[-3:]
    z = z_ref[0]
    rows = own_ref.shape[0]
    span = total - LAG
    inner = jnp.logical_or(z == 1, z == 2)
    last = jnp.where(inner, inner_ref[...].astype(jnp.float32), outer_ref[...].astype(jnp.float32))
    blocks = [own_ref[...].astype(jnp.float32), near_ref[...].astype(jnp.float32), far_ref[...].astype(jnp.float32), last]
    mean = sum(jnp.sum(block, axis=0, keepdims=True) for block in blocks) / total
    for k, block in enumerate(blocks):
        place = pl.multiple_of(jnp.bitwise_xor(z, k) * rows, rows)
        xs[pl.ds(place, rows), :] = (block - mean).astype(jnp.bfloat16)
    inst_ref[...] = jnp.dot(st_ref[...], xs[...], preferred_element_type=jnp.float32) / total
    lagged = jnp.dot(lt_ref[:, :span], xs[LAG:, :], preferred_element_type=jnp.float32)
    lagged += jnp.dot(lt_ref[:, span:], xs[:span, :], preferred_element_type=jnp.float32)
    lag_ref[...] = lagged * scale_ref[0]


def chunk_call(base, steps, z, scale, st, lt, frames, received, outs):
    rows, total = st.shape
    depth, columns = frames.shape
    width = steps * BLOCK
    smem = pl.BlockSpec(memory_space=pltpu.SMEM)
    whole = lambda a: pl.BlockSpec(a.shape, lambda j: (0, 0), pipeline_mode=pl.Buffered(1))
    part = pl.BlockSpec((depth, BLOCK), lambda j: (0, j))
    out_spec = pl.BlockSpec((rows, BLOCK), lambda j: (0, base + j))
    shape = jax.ShapeDtypeStruct((rows, columns), jnp.float32)
    operands = [z, scale, st, lt, frames, *received, *outs]
    specs = [smem, smem, whole(st), whole(lt), pl.BlockSpec((depth, BLOCK), lambda j: (0, base + j))]
    specs += [part] * len(received) + [pl.BlockSpec(memory_space=pl.ANY)] * len(outs)
    first = len(operands) - len(outs)
    flops = 2 * rows * width * (total + 2 * (total - LAG))
    return pl.pallas_call(
        functools.partial(chunk_kernel, total),
        out_shape=(shape, shape),
        grid=(steps,),
        in_specs=specs,
        out_specs=(out_spec, out_spec),
        scratch_shapes=[pltpu.VMEM((total, BLOCK), jnp.bfloat16)],
        input_output_aliases={first + k: k for k in range(len(outs))},
        cost_estimate=pl.CostEstimate(flops=flops, bytes_accessed=8 * rows * width + 5 * 2**20, transcendentals=0),
        compiler_params=pltpu.CompilerParams(vmem_limit_bytes=24 * 2**20),
    )(*operands)


def spread(value, axis):
    return lax.all_to_all(value, axis, split_axis=0, concat_axis=0, tiled=False)


def slab_rows(frames, start):
    depth, columns = frames.shape
    tiles, times = lax.axis_size("tile"), lax.axis_size("tm")
    piece = S // tiles // times
    at = jnp.clip(start - lax.axis_index("tile") * columns + S, 0, columns + S)
    padded = jnp.pad(frames, ((0, 0), (S, S)))
    mine = lax.dynamic_slice_in_dim(padded, at, S, 1)
    mine = mine.reshape(depth, times, tiles, piece).transpose(2, 1, 0, 3)
    mine = spread(mine, "tile")
    mine = jnp.sum(mine.astype(jnp.float32), axis=0).astype(jnp.bfloat16)
    z = lax.axis_index("tm")
    kept = [lax.dynamic_index_in_dim(mine, z, 0, keepdims=False)]
    for k in range(1, times):
        away = lax.dynamic_index_in_dim(mine, jnp.bitwise_xor(z, k), 0, keepdims=False)
        kept.append(permute(away, [(a, a ^ k) for a in range(times)]))
    mine = jnp.zeros((times, depth, piece), jnp.bfloat16)
    for k, block in enumerate(kept):
        mine = lax.dynamic_update_index_in_dim(mine, block, jnp.bitwise_xor(z, k), 0)
    values = mine.reshape(times * depth, piece).astype(jnp.float32)
    mean = jnp.sum(values, axis=0) / (times * depth)
    centered = (values - mean).astype(jnp.bfloat16).T
    every = jnp.broadcast_to(centered[None], (tiles, piece, times * depth))
    return spread(every, "tile").reshape(S // times, times * depth)


def chunk_units(columns):
    units = columns // BLOCK
    if units == sum(UNITS):
        return UNITS
    return (units - units // 3, units // 3) if units >= 3 else (units,)


def permute(value, pairs):
    return lax.ppermute(value, "tm", pairs)


def shards(frames, segments, offset):
    columns = frames.shape[1]
    total = segments.shape[0]
    z = lax.axis_index("tm").astype(jnp.int32).reshape(1)
    span = total - LAG
    received = []
    first = 0
    for units in chunk_units(columns):
        own = frames[:, first * BLOCK:(first + units) * BLOCK]
        far = permute(own, [(0, 2), (2, 0), (1, 3), (3, 1)])
        near = permute(own, [(0, 1), (1, 0), (2, 3), (3, 2)])
        inner = permute(own, [(1, 2), (2, 1)])
        outer = permute(far, [(1, 0), (2, 3)])
        received.append((first, units, (near, far, inner, outer)))
        first += units
    st = slab_rows(frames, offset[0])
    valid = (segments[:span] == segments[LAG:]).astype(jnp.bfloat16)
    pairs = jnp.sum(valid.astype(jnp.float32))
    lt = jnp.concatenate([st[:, :span] * valid, st[:, LAG:] * valid], axis=1)
    scale = (0.5 / pairs).reshape(1)
    outs = ()
    for first, units, parts in received:
        outs = chunk_call(first, units, z, scale, st, lt, frames, parts, outs)
    return tuple(outs)


def solution(mesh):
    in_specs = (P("tm", "tile"), P(), P())
    out_specs = (P("tm", "tile"), P("tm", "tile"))
    return jax.shard_map(shards, mesh=mesh, in_specs=in_specs, out_specs=out_specs, check_vma=False)
```
